256 devices in a mesh: band: 64 (over z, y, x_lo), slab: 4 (over x_hi, core).
Axes of the slice: x: 4 (x_hi: 2, x_lo: 2; x = x_hi * 2 + x_lo), y: 4, z: 8, core: 2. Of those that a mesh axis runs over, the one named last changes fastest.
Arguments:
- bands: float32 [256, 32, 24, 128], P('band', 'slab'), may hold values from -8 to 8
- potential: float32 [32, 24, 128], P('slab'), may hold values from -1 to 0
Outputs:
- filtered: float32 [256, 32, 24, 128], P('band', 'slab')
- correlation: float32 [256, 256], P('band')
- projected: float32 [256, 256], P('band')
The draws below stay inside these ranges and needn't reach their ends.
All inputs are finite; a program needn't handle non-finite values.
Results may differ from the reference program's by a relative error of at most 0.000092.
Values sent between devices are 32-bit elements; how exact they have to be, the bound alone decides.
No kernel may reach another device: no remote copies, remote signals or barrier semaphores. Data moves between devices by JAX's collectives and lax.ppermute only.
A program may use at most 128 MiB of HBM per device.

```python
import jax
import jax.numpy as jnp
from jax import lax

BANDS = 256
NY = 24
NX = 128
NZ = 32


def draw_bands(key, part):
    base = jax.random.fold_in(key, 11)
    first, second, third = jax.random.split(base, 3)
    common = jax.random.normal(second, (1, NZ, NY, NX), jnp.float32)
    mixing = jax.random.uniform(third, (BANDS, 1, 1, 1), jnp.float32, 0.3, 1.0)
    noise = jax.random.normal(first, (BANDS, NZ, NY, NX), jnp.float32)
    values = noise + mixing * common
    return jnp.clip(values, -8.0, 8.0)


def shard_levels(stream_key, shape, shards, least, largest):
    gain, own = 1.0, jax.random.fold_in(stream_key, 6)
    for position, parts in shards:
        steps = jnp.exp(jax.random.uniform(jax.random.fold_in(own, position), (parts,), jnp.float32, least / len(shards), largest / len(shards)))
        gain = gain * jnp.repeat(steps, shape[position] // parts).reshape([-1 if axis == position else 1 for axis in range(len(shape))])
    return gain


def setup_inputs(seed: int = 0) -> dict:
    streams_of = jax.random.split(jax.random.key(seed), 3)
    bands = draw_bands(jax.random.fold_in(streams_of[2], 71), 0)
    potential = jnp.clip(-1.0 + 1.0 * jax.random.uniform(streams_of[1], (NZ, NY, NX), jnp.float32) ** shard_levels(streams_of[1], (NZ, NY, NX), ((0, 4),), -0.2, 0.2), -1.0, 0.0)
    return {"bands": bands, "potential": potential}


centre = 4.5
half = 3.5


def hamiltonian(field, potential):
    lap = jnp.zeros_like(field)
    for axis in (1, 2, 3):
        lap = lap - 2.5 * field
        lap = lap + (4.0 / 3.0) * (jnp.roll(field, 1, axis) + jnp.roll(field, -1, axis))
        lap = lap - (1.0 / 12.0) * (jnp.roll(field, 2, axis) + jnp.roll(field, -2, axis))
    return -0.5 * lap + potential[None] * field


def reference(bands, potential):
    previous = bands
    current = (hamiltonian(bands, potential) - centre * bands) / half
    for step in range(3):
        following = 2.0 * (hamiltonian(current, potential) - centre * current) / half - previous
        previous, current = current, following
    image = hamiltonian(current, potential)
    volume = 1.0 / (NX * NY * NZ)
    flat = current.reshape(BANDS, -1)
    himage = image.reshape(BANDS, -1)
    correlation = jnp.dot(flat, flat.T, precision=lax.Precision.HIGHEST, preferred_element_type=jnp.float32) * volume
    projected = jnp.dot(himage, flat.T, precision=lax.Precision.HIGHEST, preferred_element_type=jnp.float32) * volume
    return current, correlation, projected
```

```python
import jax
import jax.numpy as jnp
from jax import lax
from jax.experimental import pallas as pl
from jax.experimental.pallas import tpu as pltpu
from jax.sharding import Mesh, PartitionSpec as P

centre = 4.5
half = 3.5

VMEM = pl.BlockSpec(memory_space=pltpu.VMEM)


def filter_kernel(bands_ref, pot_ref, filt_ref, send_ref, a_ref, b_ref, w_ref):
    nz, ny, nx = bands_ref.shape
    unroll = 4

    def wrap(ref):
        ref[0:2] = ref[nz : nz + 2]
        ref[nz + 2 : nz + 4] = ref[2:4]

    def sums(ref, z):
        v = ref[z + 2]
        one = ref[z + 1] + ref[z + 3]
        two = ref[z] + ref[z + 4]
        for axis, size in ((0, ny), (1, nx)):
            one = one + (pltpu.roll(v, 1, axis) + pltpu.roll(v, size - 1, axis))
            two = two + (pltpu.roll(v, 2, axis) + pltpu.roll(v, size - 2, axis))
        return v, one, two

    a_ref[2 : nz + 2] = bands_ref[...]
    wrap(a_ref)
    scale = 2.0 / half
    w_ref[...] = (pot_ref[...] + (3.75 - centre)) * scale

    def first(z, carry):
        v, one, two = sums(a_ref, z)
        full = w_ref[z] * v - (scale * 2.0 / 3.0) * one + (scale / 24.0) * two
        b_ref[z + 2] = 0.5 * full
        return carry

    lax.fori_loop(0, nz, first, 0, unroll=unroll)
    wrap(b_ref)
    current, previous = b_ref, a_ref
    for step in range(3):

        def advance(z, carry, current=current, previous=previous):
            v, one, two = sums(current, z)
            full = w_ref[z] * v - (scale * 2.0 / 3.0) * one + (scale / 24.0) * two
            previous[z + 2] = full - previous[z + 2]
            return carry

        lax.fori_loop(0, nz, advance, 0, unroll=unroll)
        wrap(previous)
        current, previous = previous, current

    image_ref = w_ref

    def last(z, carry):
        v, one, two = sums(current, z)
        filt_ref[z] = v
        image_ref[z] = (pot_ref[z] + 3.75) * v - (2.0 / 3.0) * one + (1.0 / 24.0) * two
        return carry

    lax.fori_loop(0, nz, last, 0, unroll=unroll)

    def pack(z, carry):
        for k in range(3):
            rows = pl.ds(k, 8, stride=3)
            send_ref[pl.ds(z * 48 + 2 * k, 8, stride=6), :] = filt_ref.at[z][rows, :]
            send_ref[pl.ds(z * 48 + 2 * k + 1, 8, stride=6), :] = image_ref.at[z][rows, :]
        return carry

    lax.fori_loop(0, nz, pack, 0, unroll=unroll)


def gram_kernel(planes, recv_ref, out_ref):
    count = recv_ref.shape[0] // 6
    across = count // planes
    filt = jnp.concatenate(
        [recv_ref[pl.ds(2 * k, count, stride=6), :] for k in range(3)], axis=1
    )
    image = jnp.concatenate(
        [recv_ref[pl.ds(2 * k + 1, count, stride=6), :] for k in range(3)], axis=1
    )
    for f, left in enumerate((filt, image)):
        block = lax.dot_general(
            left,
            filt,
            (((1,), (1,)), ((), ())),
            precision=lax.Precision.HIGHEST,
            preferred_element_type=jnp.float32,
        )
        for z in range(planes):
            for c in range(2):
                part = block[z * across : (z + 1) * across, c * 128 : (c + 1) * 128]
                out_ref[pl.ds((z * 2 + f) * 2 + c, across, stride=4 * planes), :] = part


def spread_kernel(recv_ref, out_ref):
    total = jnp.sum(recv_ref[...], axis=0)
    planes = total.shape[0] // 4
    for z in range(planes):
        for s in range(4):
            out_ref[z * 4 + s] = total[z * 4 : (z + 1) * 4]


def finish_kernel(volume, recv_ref, corr_ref, proj_ref):
    total = jnp.sum(recv_ref[...], axis=0) * volume
    for s in range(4):
        for c in range(2):
            lanes = slice(c * 128, (c + 1) * 128)
            corr_ref[s : s + 1, lanes] = total[s * 4 + c : s * 4 + c + 1]
            proj_ref[s : s + 1, lanes] = total[s * 4 + 2 + c : s * 4 + 3 + c]


def shape(*dims):
    return jax.ShapeDtypeStruct(dims, jnp.float32)


def body(bands, potential):
    slabs = lax.axis_size("slab")
    planes = lax.axis_size("z")
    across = lax.axis_size("y") * lax.axis_size("x") * slabs
    devices = planes * across
    _, thick, ny, nx = bands.shape
    nz = thick * slabs

    mine = lax.all_to_all(bands, "slab", 0, 0)
    spread = jnp.broadcast_to(potential[None], (slabs, *potential.shape))
    pot = lax.all_to_all(spread, "slab", 0, 0)

    filt, send = pl.pallas_call(
        filter_kernel,
        name="filter",
        out_shape=(shape(nz, ny, nx), shape(devices * 6, nx)),
        in_specs=[VMEM, VMEM],
        out_specs=(VMEM, VMEM),
        scratch_shapes=[
            pltpu.VMEM((nz + 4, ny, nx), jnp.float32),
            pltpu.VMEM((nz + 4, ny, nx), jnp.float32),
            pltpu.VMEM((nz, ny, nx), jnp.float32),
        ],
    )(mine.reshape(nz, ny, nx), pot.reshape(nz, ny, nx))

    recv = lax.all_to_all(send.reshape(devices, 3, 2, nx), ("z", "y", "x", "slab"), 0, 0)
    filtered = lax.all_to_all(filt.reshape(slabs, thick, ny, nx), "slab", 0, 0)

    parts = pl.pallas_call(
        lambda *refs: gram_kernel(planes, *refs),
        name="gram",
        out_shape=shape(across * 4 * planes, 128),
        in_specs=[VMEM],
        out_specs=VMEM,
    )(recv.reshape(devices * 6, nx))

    plane = lax.all_to_all(
        parts.reshape(across, 4 * planes, 128), ("y", "x", "slab"), 0, 0
    )
    rows = pl.pallas_call(
        spread_kernel,
        name="spread",
        out_shape=shape(planes * slabs, 4, 128),
        in_specs=[VMEM],
        out_specs=VMEM,
    )(plane)
    whole = lax.all_to_all(rows, ("z", "slab"), 0, 0)
    volume = 1.0 / (nz * ny * nx)
    correlation, projected = pl.pallas_call(
        lambda *refs: finish_kernel(volume, *refs),
        name="finish",
        out_shape=(shape(slabs, 2 * 128), shape(slabs, 2 * 128)),
        in_specs=[VMEM],
        out_specs=(VMEM, VMEM),
    )(whole.reshape(planes, slabs * 4, 128))
    return filtered, correlation, projected


def solution(mesh):
    bands, slabs = mesh.devices.shape
    fine = Mesh(mesh.devices.reshape(bands // 8, 4, 2, slabs), ("z", "y", "x", "slab"))
    along = ("z", "y", "x")
    in_specs = (P(along, "slab", None, None), P("slab", None, None))
    out_specs = (P(along, "slab", None, None), P(along, None), P(along, None))
    return jax.shard_map(body, mesh=fine, in_specs=in_specs, out_specs=out_specs, check_vma=False)
```

```python
import jax
import jax.numpy as jnp
from jax import lax
from jax.experimental import pallas as pl
from jax.experimental.pallas import tpu as pltpu
from jax.sharding import Mesh, PartitionSpec as P

centre = 4.5
half = 3.5
scale = 2.0 / half

VMEM = pl.BlockSpec(memory_space=pltpu.VMEM)


def neighbours(v):
    one, two = [], []
    for axis in (0, 1):
        size = v.shape[axis]
        one.append(pltpu.roll(v, 1, axis) + pltpu.roll(v, size - 1, axis))
        two.append(pltpu.roll(v, 2, axis) + pltpu.roll(v, size - 2, axis))
    return one[0] + one[1], two[0] + two[1]


def stencil(at, z):
    v = at(z)
    one, two = neighbours(v)
    one = one + (at(z - 1) + at(z + 1))
    two = two + (at(z - 2) + at(z + 2))
    return v, one, two


def pack(send_ref, at, band, z, bands):
    ny = at.shape[0]
    per = ny // 3
    for k in range(3):
        start = (z * per * bands + band) * 3 + k
        send_ref[pl.ds(start, per, stride=3 * bands), :] = at[pl.ds(k, per, stride=3), :]


def filter_kernel(
    low_ref, mid_ref, high_ref, plow_ref, pmid_ref, phigh_ref,
    filt_ref, send_ref, first_ref, last_ref,
    a_ref, b_ref, w_ref,
):
    bands, thick = mid_ref.shape[:2]
    for z in range(thick):
        for ref, base in ((plow_ref, 0), (pmid_ref, thick), (phigh_ref, 2 * thick)):
            if 2 <= base + z < 3 * thick - 2:
                w_ref[base + z] = (ref[z] + (3.75 - centre)) * scale

    def one_band(band, carry):
        def start(z):
            ref = (low_ref, mid_ref, high_ref)[z // thick]
            return ref[band, z % thick]

        def held(ref):
            return lambda z: ref[z]

        def step(at, z):
            v, one, two = stencil(at, z)
            return w_ref[z] * v - (scale * 2.0 / 3.0) * one + (scale / 24.0) * two

        for z in range(2, 3 * thick - 2):
            a_ref[z] = 0.5 * step(start, z)
        for z in range(4, 3 * thick - 4):
            b_ref[z] = step(held(a_ref), z) - start(z)
        for z in range(6, 3 * thick - 6):
            a_ref[z] = step(held(b_ref), z) - a_ref[z]
        for z in range(thick):
            new = step(held(a_ref), z + thick) - b_ref[z + thick]
            filt_ref[band, z] = new
            if z < 2:
                first_ref[band, z] = new
            if z >= thick - 2:
                last_ref[band, z - thick + 2] = new
        for z in range(thick):
            pack(send_ref, filt_ref.at[band, z], band, z, bands)
        return carry

    lax.fori_loop(0, bands, one_band, 0)


def image_kernel(filt_ref, pot_ref, low_ref, high_ref, send_ref, image_ref):
    bands, thick = filt_ref.shape[:2]

    def one_band(band, carry):
        def at(z):
            if z < 0:
                return low_ref[band, z + 2]
            return filt_ref[band, z] if z < thick else high_ref[band, z - thick]

        for z in range(thick):
            v, one, two = stencil(at, z)
            image_ref[z] = (pot_ref[z] + 3.75) * v - (2.0 / 3.0) * one + (1.0 / 24.0) * two
        for z in range(thick):
            pack(send_ref, image_ref.at[z], band, z, bands)
        return carry

    lax.fori_loop(0, bands, one_band, 0)


def columns(ref):
    count = ref.shape[0] // 3
    return jnp.concatenate([ref[pl.ds(k, count, stride=3), :] for k in range(3)], axis=1)


def product(planes, f, left, right, out_ref):
    across = left.shape[0] // planes
    block = lax.dot_general(
        left,
        right,
        (((1,), (1,)), ((), ())),
        precision=lax.Precision.HIGHEST,
        preferred_element_type=jnp.float32,
    )
    for z in range(planes):
        for c in range(2):
            part = block[z * across : (z + 1) * across, c * 128 : (c + 1) * 128]
            out_ref[pl.ds((z * 2 + f) * 2 + c, across, stride=4 * planes), :] = part


def gram_kernel(planes, filt_ref, out_ref):
    filt = columns(filt_ref)
    out_ref[...] = jnp.zeros_like(out_ref)
    product(planes, 0, filt, filt, out_ref)


def project_kernel(planes, filt_ref, image_ref, half_ref, out_ref):
    del half_ref
    product(planes, 1, columns(image_ref), columns(filt_ref), out_ref)


def spread_kernel(recv_ref, out_ref):
    total = jnp.sum(recv_ref[...], axis=0)
    planes = total.shape[0] // 4
    for z in range(planes):
        for s in range(4):
            out_ref[z * 4 + s] = total[z * 4 : (z + 1) * 4]


def finish_kernel(volume, recv_ref, corr_ref, proj_ref):
    total = jnp.sum(recv_ref[...], axis=0) * volume
    for s in range(4):
        for c in range(2):
            lanes = slice(c * 128, (c + 1) * 128)
            corr_ref[s : s + 1, lanes] = total[s * 4 + c : s * 4 + c + 1]
            proj_ref[s : s + 1, lanes] = total[s * 4 + 2 + c : s * 4 + 3 + c]


def shape(*dims):
    return jax.ShapeDtypeStruct(dims, jnp.float32)


def call(kernel, name, outs, scratch=(), **options):
    one = not isinstance(outs, tuple)

    def run(*args):
        return pl.pallas_call(
            kernel,
            name=name,
            out_shape=outs,
            in_specs=[VMEM] * len(args),
            out_specs=VMEM if one else (VMEM,) * len(outs),
            scratch_shapes=[pltpu.VMEM(dims, jnp.float32) for dims in scratch],
            compiler_params=pltpu.CompilerParams(vmem_limit_bytes=16 * 2**20),
            **options,
        )(*args)

    return run


def body(bands, potential):
    slabs = lax.axis_size("slab")
    planes = lax.axis_size("z")
    across = lax.axis_size("y") * lax.axis_size("x") * slabs
    groups = planes * across // slabs
    count, thick, ny, nx = bands.shape
    up = [(i, (i + 1) % slabs) for i in range(slabs)]
    down = [(i, (i - 1) % slabs) for i in range(slabs)]
    rows = count * thick * ny

    plow = lax.ppermute(potential, "slab", up)
    phigh = lax.ppermute(potential, "slab", down)
    low = lax.ppermute(bands, "slab", up)
    high = lax.ppermute(bands, "slab", down)

    edge = shape(count, 2, ny, nx)
    filtered, send, first, last = call(
        filter_kernel,
        "filter",
        (shape(*bands.shape), shape(rows, nx), edge, edge),
        [(3 * thick, ny, nx)] * 3,
    )(low, bands, high, plow, potential, phigh)
    below = lax.ppermute(last, "slab", up)
    above = lax.ppermute(first, "slab", down)

    def exchange(x):
        swapped = lax.all_to_all(x.reshape(groups, -1, 2, nx), ("z", "y", "x"), 0, 0)
        return swapped.reshape(rows, nx)

    filt = exchange(send)
    image = exchange(
        call(image_kernel, "image", shape(rows, nx), [(thick, ny, nx)])(
            filtered, potential, below, above
        )
    )

    parts = shape(across * 4 * planes, 128)
    half_parts = call(lambda *refs: gram_kernel(planes, *refs), "gram", parts)(filt)
    both = call(
        lambda *refs: project_kernel(planes, *refs),
        "project",
        parts,
        input_output_aliases={2: 0},
    )(filt, image, half_parts)

    plane = lax.all_to_all(both.reshape(across, 4 * planes, 128), ("y", "x", "slab"), 0, 0)
    sums = call(spread_kernel, "spread", shape(planes * slabs, 4, 128))(plane)
    whole = lax.all_to_all(sums, ("z", "slab"), 0, 0)
    volume = 1.0 / (slabs * thick * ny * nx)
    correlation, projected = call(
        lambda *refs: finish_kernel(volume, *refs),
        "finish",
        (shape(slabs, 2 * 128), shape(slabs, 2 * 128)),
    )(whole.reshape(planes, slabs * 4, 128))
    return filtered, correlation, projected


def solution(mesh):
    bands, slabs = mesh.devices.shape
    fine = Mesh(mesh.devices.reshape(bands // 8, 4, 2, slabs), ("z", "y", "x", "slab"))
    along = ("z", "y", "x")
    in_specs = (P(along, "slab", None, None), P("slab", None, None))
    out_specs = (P(along, "slab", None, None), P(along, None), P(along, None))
    return jax.shard_map(body, mesh=fine, in_specs=in_specs, out_specs=out_specs, check_vma=False)
```

```python
import jax
import jax.numpy as jnp
from jax import lax
from jax.experimental import pallas as pl
from jax.experimental.pallas import tpu as pltpu
from jax.sharding import Mesh, PartitionSpec as P


centre = 4.5
half = 3.5
scale = 2.0 / half

VMEM = pl.BlockSpec(memory_space=pltpu.VMEM)


def neighbours(v):
    one, two = [], []
    for axis in (0, 1):
        size = v.shape[axis]
        one.append(pltpu.roll(v, 1, axis) + pltpu.roll(v, size - 1, axis))
        two.append(pltpu.roll(v, 2, axis) + pltpu.roll(v, size - 2, axis))
    return one[0] + one[1], two[0] + two[1]


def stencil(at, z):
    v = at(z)
    one, two = neighbours(v)
    one = one + (at(z - 1) + at(z + 1))
    two = two + (at(z - 2) + at(z + 2))
    return v, one, two


def filter_kernel(odd_ref, near_ref, mid_ref, far_ref, ends_ref, pnear_ref, pmid_ref, pfar_ref, *rest):
    odd = odd_ref[0]

    @pl.when(odd == 0)
    def _():
        filter_bands(far_ref, mid_ref, near_ref, ends_ref, pfar_ref, pmid_ref, pnear_ref, *rest)

    @pl.when(odd == 1)
    def _():
        filter_bands(near_ref, mid_ref, far_ref, ends_ref, pnear_ref, pmid_ref, pfar_ref, *rest)


def filter_bands(
    low_ref, mid_ref, high_ref, far_ref, plow_ref, pmid_ref, phigh_ref,
    filt_ref, send_ref,
    a_ref, b_ref, image_ref, weight_ref,
):
    bands, thick = mid_ref.shape[:2]
    edge = far_ref.shape[1] // 2
    total = 3 * thick + 2 * edge
    own = thick + edge

    for part, ref in enumerate((plow_ref, pmid_ref, phigh_ref)):
        for z in range(thick):
            weight_ref[edge + part * thick + z] = (ref[z] + (3.75 - centre)) * scale

    def one_band(band, carry):
        def start(z):
            z = z - edge
            if z < 0:
                return far_ref[band, z + 2 * edge]
            if z >= 3 * thick:
                return far_ref[band, z - 3 * thick]
            return (low_ref, mid_ref, high_ref)[z // thick][band, z % thick]

        def held(ref):
            return lambda z: ref[z]

        def step(at, z):
            v, one, two = stencil(at, z)
            return v, weight_ref[z] * v - (scale * 2.0 / 3.0) * one + (scale / 24.0) * two

        for z in range(2, total - 2):
            a_ref[z] = 0.5 * step(start, z)[1]
        for z in range(4, total - 4):
            b_ref[z] = step(held(a_ref), z)[1] - start(z)
        for z in range(6, total - 6):
            a_ref[z] = step(held(b_ref), z)[1] - a_ref[z]
        for z in range(8, total - 8):
            new = step(held(a_ref), z)[1] - b_ref[z]
            b_ref[z] = new
            if own <= z < own + thick:
                filt_ref[band, z - own] = new
        for z in range(thick):
            v, full = step(held(b_ref), z + own)
            image_ref[z] = (0.5 * half) * full + centre * v
        per = image_ref.shape[1] // 3
        for z in range(thick):
            for f, at in enumerate((filt_ref.at[band, z], image_ref.at[z])):
                for k in range(3):
                    first = ((z * per * bands + band) * 2 + f) * 3 + k
                    send_ref[pl.ds(first, per, stride=6 * bands), :] = at[pl.ds(k, per, stride=3), :]
        return carry

    lax.fori_loop(0, bands, one_band, 0)


def gram_kernel(planes, per_chunk, *refs):
    recv_refs, out_ref, held = refs[:-7], refs[-7], refs[-6:]
    size = held[0].shape[0]
    bands = per_chunk * len(recv_refs)
    groups = size // bands
    across = size // planes
    for f in range(2):
        for k in range(3):
            for band in range(bands):
                ref = recv_refs[band // per_chunk]
                first = ((band % per_chunk) * 2 + f) * 3 + k
                part = ref[pl.ds(first, groups, stride=6 * per_chunk), :]
                held[f * 3 + k][pl.ds(band, groups, stride=bands), :] = part
    filt = jnp.concatenate([ref[...] for ref in held[:3]], axis=1)
    image = jnp.concatenate([ref[...] for ref in held[3:]], axis=1)
    for f, left in enumerate((filt, image)):
        block = lax.dot_general(
            left,
            filt,
            (((1,), (1,)), ((), ())),
            precision=lax.Precision.HIGHEST,
            preferred_element_type=jnp.float32,
        )
        for z in range(planes):
            for c in range(2):
                part = block[z * across : (z + 1) * across, c * 128 : (c + 1) * 128]
                out_ref[pl.ds((z * 2 + f) * 2 + c, across, stride=4 * planes), :] = part


def spread_kernel(recv_ref, out_ref):
    total = jnp.sum(recv_ref[...], axis=0)
    planes = total.shape[0] // 4
    for z in range(planes):
        for s in range(4):
            out_ref[z * 4 + s] = total[z * 4 : (z + 1) * 4]


def finish_kernel(volume, recv_ref, corr_ref, proj_ref):
    total = jnp.sum(recv_ref[...], axis=0) * volume
    for s in range(4):
        for c in range(2):
            lanes = slice(c * 128, (c + 1) * 128)
            corr_ref[s : s + 1, lanes] = total[s * 4 + c : s * 4 + c + 1]
            proj_ref[s : s + 1, lanes] = total[s * 4 + 2 + c : s * 4 + 3 + c]


def shape(*dims):
    return jax.ShapeDtypeStruct(dims, jnp.float32)


def call(kernel, outs, scratch=(), scalars=0):
    one = not isinstance(outs, tuple)

    def run(*args):
        return pl.pallas_call(
            kernel,
            out_shape=outs,
            in_specs=[pl.BlockSpec(memory_space=pltpu.SMEM)] * scalars + [VMEM] * (len(args) - scalars),
            out_specs=VMEM if one else (VMEM,) * len(outs),
            scratch_shapes=[pltpu.VMEM(dims, jnp.float32) for dims in scratch],
            compiler_params=pltpu.CompilerParams(vmem_limit_bytes=16 * 2**20),
        )(*args)

    return run


CHUNKS = 1


def work(bands, potential):
    slabs = lax.axis_size("slab")
    planes = lax.axis_size("z")
    across = lax.axis_size("y") * lax.axis_size("x") * slabs
    groups = planes * across // slabs
    count, thick, ny, nx = bands.shape
    near = [(0, 1), (1, 0), (2, 3), (3, 2)]
    far = [(0, 3), (3, 0), (1, 2), (2, 1)]
    odd = jnp.reshape(lax.axis_index("slab") % 2, (1,)).astype(jnp.int32)
    each = count // CHUNKS
    rows = each * 2 * thick * ny

    pieces = []
    for chunk in range(CHUNKS):
        mid = bands[chunk * each : (chunk + 1) * each]
        other = lax.ppermute(mid, "slab", far)
        beside = lax.ppermute(mid, "slab", near)
        ends = jnp.concatenate([other[:, :2], other[:, -2:]], axis=1)
        ends = lax.ppermute(ends, "slab", near)
        pieces.append((beside, mid, other, ends))
    pfar = lax.ppermute(potential, "slab", far)
    pnear = lax.ppermute(potential, "slab", near)

    filtered, received = [], []
    for piece in pieces:
        filt, send = call(
            filter_kernel,
            (shape(each, thick, ny, nx), shape(rows, nx)),
            [(3 * thick + 4, ny, nx)] * 2 + [(thick, ny, nx), (3 * thick + 4, ny, nx)],
            scalars=1,
        )(odd, *piece, pnear, potential, pfar)
        swapped = lax.all_to_all(send.reshape(groups, -1, 2, nx), ("z", "y", "x"), 0, 0)
        filtered.append(filt)
        received.append(swapped.reshape(rows, nx))

    size = groups * count
    parts = call(
        lambda *refs: gram_kernel(planes, each, *refs),
        shape(across * 4 * planes, 128),
        [(size, nx)] * 6,
    )(*received)

    plane = lax.all_to_all(parts.reshape(across, 4 * planes, 128), ("y", "x", "slab"), 0, 0)
    sums = call(spread_kernel, shape(planes * slabs, 4, 128))(plane)
    whole = lax.all_to_all(sums, ("z", "slab"), 0, 0)
    volume = 1.0 / (slabs * thick * ny * nx)
    correlation, projected = call(
        lambda *refs: finish_kernel(volume, *refs), (shape(slabs, 2 * 128), shape(slabs, 2 * 128))
    )(whole.reshape(planes, slabs * 4, 128))
    return jnp.concatenate(filtered, axis=0), correlation, projected


def solution(mesh):
    bands, slabs = mesh.devices.shape
    fine = Mesh(mesh.devices.reshape(bands // 8, 4, 2, slabs), ("z", "y", "x", "slab"))
    along = ("z", "y", "x")
    in_specs = (P(along, "slab", None, None), P("slab", None, None))
    out_specs = (P(along, "slab", None, None), P(along, None), P(along, None))
    return jax.shard_map(work, mesh=fine, in_specs=in_specs, out_specs=out_specs, check_vma=False)
```

```python
import jax
import jax.numpy as jnp
from jax import lax
from jax.experimental import pallas as pl
from jax.experimental.pallas import tpu as pltpu
from jax.sharding import Mesh, PartitionSpec as P


centre = 4.5
half = 3.5
scale = 2.0 / half

VMEM = pl.BlockSpec(memory_space=pltpu.VMEM)


def neighbours(v):
    one, two = [], []
    for axis in (0, 1):
        size = v.shape[axis]
        one.append(pltpu.roll(v, 1, axis) + pltpu.roll(v, size - 1, axis))
        two.append(pltpu.roll(v, 2, axis) + pltpu.roll(v, size - 2, axis))
    return one[0] + one[1], two[0] + two[1]


def stencil(at, z):
    v = at(z)
    one, two = neighbours(v)
    one = one + (at(z - 1) + at(z + 1))
    two = two + (at(z - 2) + at(z + 2))
    return v, one, two


def filter_kernel(odd_ref, near_ref, mid_ref, far_ref, ends_ref, pnear_ref, pmid_ref, pfar_ref, *rest):
    odd = odd_ref[0]

    @pl.when(odd == 0)
    def _():
        filter_bands(far_ref, mid_ref, near_ref, ends_ref, pfar_ref, pmid_ref, pnear_ref, *rest)

    @pl.when(odd == 1)
    def _():
        filter_bands(near_ref, mid_ref, far_ref, ends_ref, pnear_ref, pmid_ref, pfar_ref, *rest)


def filter_bands(
    low_ref, mid_ref, high_ref, far_ref, plow_ref, pmid_ref, phigh_ref,
    filt_ref, send_ref,
    a_ref, b_ref, image_ref, weight_ref,
):
    bands, thick = mid_ref.shape[:2]
    edge = far_ref.shape[1] // 2
    total = 3 * thick + 2 * edge
    own = thick + edge

    for part, ref in enumerate((plow_ref, pmid_ref, phigh_ref)):
        for z in range(thick):
            weight_ref[edge + part * thick + z] = (ref[z] + (3.75 - centre)) * scale

    def one_band(band, carry):
        def start(z):
            z = z - edge
            if z < 0:
                return far_ref[band, z + 2 * edge]
            if z >= 3 * thick:
                return far_ref[band, z - 3 * thick]
            return (low_ref, mid_ref, high_ref)[z // thick][band, z % thick]

        def held(ref):
            return lambda z: ref[z]

        def step(at, z):
            v, one, two = stencil(at, z)
            return v, weight_ref[z] * v - (scale * 2.0 / 3.0) * one + (scale / 24.0) * two

        for z in range(2, total - 2):
            a_ref[z] = 0.5 * step(start, z)[1]
        for z in range(4, total - 4):
            b_ref[z] = step(held(a_ref), z)[1] - start(z)
        for z in range(6, total - 6):
            a_ref[z] = step(held(b_ref), z)[1] - a_ref[z]
        for z in range(8, total - 8):
            new = step(held(a_ref), z)[1] - b_ref[z]
            b_ref[z] = new
            if own <= z < own + thick:
                filt_ref[band, z - own] = new
        for z in range(thick):
            v, full = step(held(b_ref), z + own)
            image_ref[z] = (0.5 * half) * full + centre * v
        per = image_ref.shape[1] // 3
        for z in range(thick):
            for f, at in enumerate((filt_ref.at[band, z], image_ref.at[z])):
                for k in range(3):
                    first = ((z * per * bands + band) * 2 + f) * 3 + k
                    send_ref[pl.ds(first, per, stride=6 * bands), :] = at[pl.ds(k, per, stride=3), :]
        return carry

    lax.fori_loop(0, bands, one_band, 0)


def gram_kernel(per_chunk, *refs):
    recv_refs, out_ref, held = refs[:-7], refs[-7], refs[-6:]
    size = held[0].shape[0]
    bands = per_chunk * len(recv_refs)
    groups = size // bands
    for f in range(2):
        for k in range(3):
            for band in range(bands):
                ref = recv_refs[band // per_chunk]
                first = ((band % per_chunk) * 2 + f) * 3 + k
                part = ref[pl.ds(first, groups, stride=6 * per_chunk), :]
                held[f * 3 + k][pl.ds(band, groups, stride=bands), :] = part
    filt = jnp.concatenate([ref[...] for ref in held[:3]], axis=1)
    image = jnp.concatenate([ref[...] for ref in held[3:]], axis=1)
    for f, left in enumerate((filt, image)):
        block = lax.dot_general(
            left,
            filt,
            (((1,), (1,)), ((), ())),
            precision=lax.Precision.HIGHEST,
            preferred_element_type=jnp.float32,
        )
        for c in range(2):
            out_ref[pl.ds(f * 2 + c, size, stride=4), :] = block[:, c * 128 : (c + 1) * 128]


def collect_kernel(recv_ref, out_ref):
    out_ref[...] = jnp.sum(recv_ref[...], axis=0)


def finish_kernel(volume, own_ref, next_ref, over_ref, last_ref, corr_ref, proj_ref):
    total = (own_ref[...] + over_ref[...]) + (next_ref[...] + last_ref[...])
    total = total * volume
    for band in range(corr_ref.shape[0]):
        for c in range(2):
            lanes = slice(c * 128, (c + 1) * 128)
            row = band * 4 + c
            corr_ref[band : band + 1, lanes] = total[row : row + 1]
            proj_ref[band : band + 1, lanes] = total[row + 2 : row + 3]


def shape(*dims):
    return jax.ShapeDtypeStruct(dims, jnp.float32)


def call(kernel, outs, scratch=(), scalars=0):
    one = not isinstance(outs, tuple)

    def run(*args):
        return pl.pallas_call(
            kernel,
            out_shape=outs,
            in_specs=[pl.BlockSpec(memory_space=pltpu.SMEM)] * scalars + [VMEM] * (len(args) - scalars),
            out_specs=VMEM if one else (VMEM,) * len(outs),
            scratch_shapes=[pltpu.VMEM(dims, jnp.float32) for dims in scratch],
            compiler_params=pltpu.CompilerParams(vmem_limit_bytes=16 * 2**20),
        )(*args)

    return run


CHUNKS = 1


def work(bands, potential):
    slabs = lax.axis_size("slab")
    groups = lax.axis_size("z") * lax.axis_size("y") * lax.axis_size("x")
    count, thick, ny, nx = bands.shape
    near = [(0, 1), (1, 0), (2, 3), (3, 2)]
    far = [(0, 3), (3, 0), (1, 2), (2, 1)]
    odd = jnp.reshape(lax.axis_index("slab") % 2, (1,)).astype(jnp.int32)
    each = count // CHUNKS
    rows = each * 2 * thick * ny

    pieces = []
    for chunk in range(CHUNKS):
        mid = bands[chunk * each : (chunk + 1) * each]
        other = lax.ppermute(mid, "slab", far)
        beside = lax.ppermute(mid, "slab", near)
        ends = jnp.concatenate([other[:, :2], other[:, -2:]], axis=1)
        ends = lax.ppermute(ends, "slab", near)
        pieces.append((beside, mid, other, ends))
    pfar = lax.ppermute(potential, "slab", far)
    pnear = lax.ppermute(potential, "slab", near)

    filtered, received = [], []
    for piece in pieces:
        filt, send = call(
            filter_kernel,
            (shape(each, thick, ny, nx), shape(rows, nx)),
            [(3 * thick + 4, ny, nx)] * 2 + [(thick, ny, nx), (3 * thick + 4, ny, nx)],
            scalars=1,
        )(odd, *piece, pnear, potential, pfar)
        swapped = lax.all_to_all(send.reshape(groups, -1, 2, nx), ("z", "y", "x"), 0, 0)
        filtered.append(filt)
        received.append(swapped.reshape(rows, nx))

    size = groups * count
    parts = call(
        lambda *refs: gram_kernel(each, *refs), shape(size * 4, 128), [(size, nx)] * 6
    )(*received)

    swapped = lax.all_to_all(parts.reshape(groups, count * 4, 128), ("z", "y", "x"), 0, 0)
    own = call(collect_kernel, shape(count * 4, 128))(swapped)
    others = [lax.ppermute(own, "slab", [(i, (i + k) % slabs) for i in range(slabs)]) for k in (1, 2, 3)]
    volume = 1.0 / (slabs * thick * ny * nx)
    correlation, projected = call(
        lambda *refs: finish_kernel(volume, *refs), (shape(count, 2 * 128), shape(count, 2 * 128))
    )(own, *others)
    return jnp.concatenate(filtered, axis=0), correlation, projected


def solution(mesh):
    bands, slabs = mesh.devices.shape
    fine = Mesh(mesh.devices.reshape(bands // 8, 4, 2, slabs), ("z", "y", "x", "slab"))
    along = ("z", "y", "x")
    in_specs = (P(along, "slab", None, None), P("slab", None, None))
    out_specs = (P(along, "slab", None, None), P(along, None), P(along, None))
    return jax.shard_map(work, mesh=fine, in_specs=in_specs, out_specs=out_specs, check_vma=False)
```

```python
import jax
import jax.numpy as jnp
import numpy as np
from jax import lax
from jax.experimental import pallas as pl
from jax.experimental.pallas import tpu as pltpu
from jax.sharding import Mesh, PartitionSpec as P


centre = 4.5
half = 3.5
scale = 2.0 / half

VMEM = pl.BlockSpec(memory_space=pltpu.VMEM)


BLOCK = 6


def stencil_matrices(ny, nx):
    depth = -(-(BLOCK + 4) * ny // 128) * 128
    yz = np.zeros((BLOCK, ny, depth), np.float32)
    for plane in range(BLOCK):
        for y in range(ny):
            for step, weight in ((1, -16.0), (2, 1.0)):
                for sign in (-step, step):
                    yz[plane, y, (plane + 2 + sign) * ny + y] += weight
                    yz[plane, y, (plane + 2) * ny + (y + sign) % ny] += weight
    x = np.zeros((nx, nx), np.float32)
    for column in range(nx):
        for step, weight in ((1, -16.0), (2, 1.0)):
            for sign in (-step, step):
                x[(column + sign) % nx, column] += weight
    return yz.reshape(BLOCK * ny, depth), np.concatenate([x, x])


def blocks(low, high):
    return [(z, min(BLOCK, high - z)) for z in range(low, high, BLOCK)]


def filter_kernel(odd_ref, yz_ref, x_ref, near_ref, mid_ref, outer_ref, inner_ref, ends_ref, *rest):
    pnear_ref, pmid_ref, pfar_ref, *rest = rest
    thick = mid_ref.shape[1]

    def own(ref):
        return lambda band, z: ref[band, z]

    def far(band, z):
        if 2 <= z < thick - 2:
            return inner_ref[band, (z - 2) // 2, z % 2]
        return outer_ref[band, z // (thick - 2), z % 2]

    def ends(band, z):
        return ends_ref[band, z // 2, z % 2]

    odd = odd_ref[0]

    @pl.when(odd == 0)
    def _():
        fields, pots = (far, own(mid_ref), own(near_ref)), (pfar_ref, pmid_ref, pnear_ref)
        filter_bands(mid_ref.shape, yz_ref, x_ref, fields, ends, pots, *rest)

    @pl.when(odd == 1)
    def _():
        fields, pots = (own(near_ref), own(mid_ref), far), (pnear_ref, pmid_ref, pfar_ref)
        filter_bands(mid_ref.shape, yz_ref, x_ref, fields, ends, pots, *rest)


def filter_bands(
    dims, yz_ref, x_ref, fields, ends, pots,
    filt_ref, send_ref,
    field_ref, split_ref, image_ref, weight_ref,
):
    bands, thick, ny, nx = dims
    edge = 2
    total = 3 * thick + 2 * edge
    own = thick + edge
    depth = yz_ref.shape[1]
    pad = split_ref.shape[2] - total * ny

    for part, ref in enumerate(pots):
        for z in range(thick):
            top = (edge + part * thick + z) * ny
            weight_ref[top : top + ny, :] = (ref[z] + (3.75 - centre)) * scale

    def split(into, top, height, value):
        for term, part in enumerate(terms(value)):
            split_ref[into, term, top : top + height, :] = part

    blank = jnp.zeros((pad + 2 * ny, 2 * nx), jnp.bfloat16)
    for into in range(2):
        for term in range(2):
            split_ref[into, term, (total - 2) * ny :, :] = blank

    def dot(left, right):
        return jnp.dot(left, right, preferred_element_type=jnp.float32)

    def step(level, z, planes):
        source = level % 2
        window = slice((z - 2) * ny, (z - 2) * ny + depth)
        here = slice(z * ny, (z + planes) * ny)
        weights = yz_ref[: planes * ny, :]
        near = dot(weights, split_ref[source, 0, window, :])
        near = near + dot(weights, split_ref[source, 1, window, :])
        lead, rest = split_ref[source, 0, here, :], split_ref[source, 1, here, :]
        along = [
            dot(jnp.concatenate([lead[:, lanes], rest[:, lanes]], axis=1), x_ref[...])
            for lanes in (slice(0, nx), slice(nx, 2 * nx))
        ]
        near = near + jnp.concatenate(along, axis=1)
        value = field_ref[level, here, :]
        weight = weight_ref[here, :]
        weight = jnp.concatenate([weight, weight], axis=1)
        return value, weight * value + (scale / 24.0) * near

    def pair(index, carry):
        first = index * 2
        for z in range(0, total, 2):
            if z < edge:
                get, at = ends, z + edge
            elif z >= total - edge:
                get, at = ends, z - (total - edge)
            else:
                get, at = fields[(z - edge) // thick], (z - edge) % thick
            value = jnp.concatenate(
                [
                    jnp.concatenate([get(first + band, at), get(first + band, at + 1)], axis=0)
                    for band in range(2)
                ],
                axis=1,
            )
            field_ref[0, z * ny : (z + 2) * ny, :] = value
            split(0, z * ny, 2 * ny, value)
        for level in range(4):
            for z, planes in blocks(2 * level + 2, total - 2 * level - 2):
                here = slice(z * ny, (z + planes) * ny)
                full = step(level, z, planes)[1]
                new = 0.5 * full if level == 0 else full - field_ref[level - 1, here, :]
                if level < 3:
                    field_ref[level + 1, here, :] = new
                else:
                    field_ref[4, here, :] = new
                    for plane in range(max(z, own), min(z + planes, own + thick)):
                        piece = new[(plane - z) * ny : (plane - z + 1) * ny]
                        for band in range(2):
                            filt_ref[first + band, plane - own] = piece[:, band * nx : (band + 1) * nx]
                split((level + 1) % 2, z * ny, planes * ny, new)
        for z, planes in blocks(own, own + thick):
            value, full = step(4, z, planes)
            new = (0.5 * half) * full + centre * value
            for plane in range(planes):
                piece = new[plane * ny : (plane + 1) * ny]
                for band in range(2):
                    image_ref[band, z + plane - own] = piece[:, band * nx : (band + 1) * nx]
        per = ny // 3
        for band in range(2):
            for z in range(thick):
                for f, at in enumerate((filt_ref.at[first + band, z], image_ref.at[band, z])):
                    for k in range(3):
                        line = ((z * per * bands + first + band) * 2 + f) * 3 + k
                        send_ref[pl.ds(line, per, stride=6 * bands), :] = at[pl.ds(k, per, stride=3), :]
        return carry

    lax.fori_loop(0, bands // 2, pair, 0)


def terms(value):
    lead = value.astype(jnp.bfloat16)
    return lead, (value - lead.astype(jnp.float32)).astype(jnp.bfloat16)


def gram_kernel(per_chunk, *refs):
    recv_refs, out_ref, held = refs[:-7], refs[-7], refs[-6:]
    size = held[0].shape[0]
    bands = per_chunk * len(recv_refs)
    groups = size // bands
    for f in range(2):
        for k in range(3):
            for band in range(bands):
                ref = recv_refs[band // per_chunk]
                first = ((band % per_chunk) * 2 + f) * 3 + k
                part = ref[pl.ds(first, groups, stride=6 * per_chunk), :]
                held[f * 3 + k][pl.ds(band, groups, stride=bands), :] = part
    filt, image = (
        terms(jnp.concatenate([ref[...] for ref in refs], axis=1)) for refs in (held[:3], held[3:])
    )
    right = jnp.concatenate([filt[0], filt[1], filt[0]], axis=1)
    for f, (lead, rest) in enumerate((filt, image)):
        block = lax.dot_general(
            jnp.concatenate([lead, lead, rest], axis=1),
            right,
            (((1,), (1,)), ((), ())),
            preferred_element_type=jnp.float32,
        )
        for c in range(2):
            out_ref[pl.ds(f * 2 + c, size, stride=4), :] = block[:, c * 128 : (c + 1) * 128]


def collect_kernel(recv_ref, out_ref):
    out_ref[...] = jnp.sum(recv_ref[...], axis=0)


def finish_kernel(volume, own_ref, next_ref, over_ref, last_ref, corr_ref, proj_ref):
    total = (own_ref[...] + over_ref[...]) + (next_ref[...] + last_ref[...])
    total = total * volume
    for band in range(corr_ref.shape[0]):
        for c in range(2):
            lanes = slice(c * 128, (c + 1) * 128)
            row = band * 4 + c
            corr_ref[band : band + 1, lanes] = total[row : row + 1]
            proj_ref[band : band + 1, lanes] = total[row + 2 : row + 3]


def shape(*dims):
    return jax.ShapeDtypeStruct(dims, jnp.float32)


def room(dims):
    kind = jnp.float32 if isinstance(dims[-1], int) else dims[-1]
    return pltpu.VMEM(tuple(d for d in dims if isinstance(d, int)), kind)


def call(kernel, outs, scratch=(), scalars=0):
    one = not isinstance(outs, tuple)

    def run(*args):
        return pl.pallas_call(
            kernel,
            out_shape=outs,
            in_specs=[pl.BlockSpec(memory_space=pltpu.SMEM)] * scalars + [VMEM] * (len(args) - scalars),
            out_specs=VMEM if one else (VMEM,) * len(outs),
            scratch_shapes=[room(dims) for dims in scratch],
            compiler_params=pltpu.CompilerParams(vmem_limit_bytes=16 * 2**20),
        )(*args)

    return run


def work(bands, potential):
    slabs = lax.axis_size("slab")
    groups = lax.axis_size("z") * lax.axis_size("y") * lax.axis_size("x")
    count, thick, ny, nx = bands.shape
    near = [(0, 1), (1, 0), (2, 3), (3, 2)]
    far = [(0, 3), (3, 0), (1, 2), (2, 1)]
    odd = jnp.reshape(lax.axis_index("slab") % 2, (1,)).astype(jnp.int32)
    rows = count * 2 * thick * ny

    pfar = lax.ppermute(potential, "slab", far)
    paired = bands.reshape(count, thick // 2, 2, ny, nx)
    outer = lax.ppermute(paired[:, :: thick // 2 - 1], "slab", far)
    inner = lax.ppermute(paired[:, 1:-1], "slab", far)
    beside = lax.ppermute(bands, "slab", near)
    pnear = lax.ppermute(potential, "slab", near)
    ends = lax.ppermute(outer, "slab", near)

    yz, x = (jnp.asarray(m, jnp.bfloat16) for m in stencil_matrices(ny, nx))
    deep = (3 * thick + 4) * ny + 64
    filtered, send = call(
        filter_kernel,
        (shape(count, thick, ny, nx), shape(rows, nx)),
        [
            (5, deep, 2 * nx),
            (2, 2, deep, 2 * nx, jnp.bfloat16),
            (2, thick, ny, nx),
            (deep, nx),
        ],
        scalars=1,
    )(odd, yz, x, beside, bands, outer, inner, ends, pnear, potential, pfar)
    swapped = lax.all_to_all(send.reshape(groups, -1, 2, nx), ("z", "y", "x"), 0, 0)
    received = swapped.reshape(rows, nx)

    size = groups * count
    parts = call(
        lambda *refs: gram_kernel(count, *refs), shape(size * 4, 128), [(size, nx)] * 6
    )(received)

    swapped = lax.all_to_all(parts.reshape(groups, count * 4, 128), ("z", "y", "x"), 0, 0)
    own = call(collect_kernel, shape(count * 4, 128))(swapped)
    others = [lax.ppermute(own, "slab", [(i, (i + k) % slabs) for i in range(slabs)]) for k in (1, 2, 3)]
    volume = 1.0 / (slabs * thick * ny * nx)
    correlation, projected = call(
        lambda *refs: finish_kernel(volume, *refs), (shape(count, 2 * 128), shape(count, 2 * 128))
    )(own, *others)
    return filtered, correlation, projected


def solution(mesh):
    bands, slabs = mesh.devices.shape
    fine = Mesh(mesh.devices.reshape(bands // 8, 4, 2, slabs), ("z", "y", "x", "slab"))
    along = ("z", "y", "x")
    in_specs = (P(along, "slab", None, None), P("slab", None, None))
    out_specs = (P(along, "slab", None, None), P(along, None), P(along, None))
    return jax.shard_map(work, mesh=fine, in_specs=in_specs, out_specs=out_specs, check_vma=False)
```

```python
import jax
import jax.numpy as jnp
import numpy as np
from jax import lax
from jax.experimental import pallas as pl
from jax.experimental.pallas import tpu as pltpu
from jax.sharding import Mesh, PartitionSpec as P


centre = 4.5
half = 3.5
scale = 2.0 / half

VMEM = pl.BlockSpec(memory_space=pltpu.VMEM)


BLOCK = 6


def stencil_matrices(ny, nx):
    depth = -(-(BLOCK + 4) * ny // 128) * 128
    yz = np.zeros((BLOCK, ny, depth), np.float32)
    for plane in range(BLOCK):
        for y in range(ny):
            for step, weight in ((1, -16.0), (2, 1.0)):
                for sign in (-step, step):
                    yz[plane, y, (plane + 2 + sign) * ny + y] += weight
                    yz[plane, y, (plane + 2) * ny + (y + sign) % ny] += weight
    x = np.zeros((nx, nx), np.float32)
    for column in range(nx):
        for step, weight in ((1, -16.0), (2, 1.0)):
            for sign in (-step, step):
                x[(column + sign) % nx, column] += weight
    return yz.reshape(BLOCK * ny, depth), np.concatenate([x, x])


def blocks(low, high):
    return [(z, min(BLOCK, high - z)) for z in range(low, high, BLOCK)]


def filter_kernel(odd_ref, yz_ref, x_ref, near_ref, mid_ref, outer_ref, inner_ref, ends_ref, *rest):
    pnear_ref, pmid_ref, pfar_ref, *rest = rest
    thick = mid_ref.shape[1]

    def own(ref):
        return lambda band, z: ref[band, z]

    def far(band, z):
        if 2 <= z < thick - 2:
            return inner_ref[band, (z - 2) // 2, z % 2]
        return outer_ref[band, z // (thick - 2), z % 2]

    def ends(band, z):
        return ends_ref[band, z // 2, z % 2]

    odd = odd_ref[0]

    @pl.when(odd == 0)
    def _():
        fields, pots = (far, own(mid_ref), own(near_ref)), (pfar_ref, pmid_ref, pnear_ref)
        filter_bands(mid_ref.shape, yz_ref, x_ref, fields, ends, pots, *rest)

    @pl.when(odd == 1)
    def _():
        fields, pots = (own(near_ref), own(mid_ref), far), (pnear_ref, pmid_ref, pfar_ref)
        filter_bands(mid_ref.shape, yz_ref, x_ref, fields, ends, pots, *rest)


def filter_bands(
    dims, yz_ref, x_ref, fields, ends, pots,
    filt_ref, send_ref,
    field_ref, split_ref, image_ref, weight_ref,
):
    bands, thick, ny, nx = dims
    edge = 2
    total = 3 * thick + 2 * edge
    own = thick + edge
    depth = yz_ref.shape[1]
    pad = split_ref.shape[2] - total * ny

    for part, ref in enumerate(pots):
        for z in range(thick):
            top = (edge + part * thick + z) * ny
            weight_ref[top : top + ny, :] = (ref[z] + (3.75 - centre)) * scale

    def split(into, top, height, value):
        for term, part in enumerate(terms(value)):
            split_ref[into, term, top : top + height, :] = part

    blank = jnp.zeros((pad + 2 * ny, 2 * nx), jnp.bfloat16)
    for into in range(2):
        for term in range(2):
            split_ref[into, term, (total - 2) * ny :, :] = blank

    def dot(left, right):
        return jnp.dot(left, right, preferred_element_type=jnp.float32)

    def step(level, z, planes):
        source = level % 2
        window = slice((z - 2) * ny, (z - 2) * ny + depth)
        here = slice(z * ny, (z + planes) * ny)
        weights = yz_ref[: planes * ny, :]
        near = dot(weights, split_ref[source, 0, window, :])
        near = near + dot(weights, split_ref[source, 1, window, :])
        lead, rest = split_ref[source, 0, here, :], split_ref[source, 1, here, :]
        along = [
            dot(jnp.concatenate([lead[:, lanes], rest[:, lanes]], axis=1), x_ref[...])
            for lanes in (slice(0, nx), slice(nx, 2 * nx))
        ]
        near = near + jnp.concatenate(along, axis=1)
        value = field_ref[level, here, :]
        weight = weight_ref[here, :]
        weight = jnp.concatenate([weight, weight], axis=1)
        return value, weight * value + (scale / 24.0) * near

    def pair(index, carry):
        first = index * 2
        for z in range(0, total, 2):
            if z < edge:
                get, at = ends, z + edge
            elif z >= total - edge:
                get, at = ends, z - (total - edge)
            else:
                get, at = fields[(z - edge) // thick], (z - edge) % thick
            value = jnp.concatenate(
                [
                    jnp.concatenate([get(first + band, at), get(first + band, at + 1)], axis=0)
                    for band in range(2)
                ],
                axis=1,
            )
            field_ref[0, z * ny : (z + 2) * ny, :] = value
            split(0, z * ny, 2 * ny, value)
        for level in range(4):
            for z, planes in blocks(2 * level + 2, total - 2 * level - 2):
                here = slice(z * ny, (z + planes) * ny)
                full = step(level, z, planes)[1]
                new = 0.5 * full if level == 0 else full - field_ref[level - 1, here, :]
                if level < 3:
                    field_ref[level + 1, here, :] = new
                else:
                    field_ref[4, here, :] = new
                    for plane in range(max(z, own), min(z + planes, own + thick)):
                        piece = new[(plane - z) * ny : (plane - z + 1) * ny]
                        for band in range(2):
                            filt_ref[first + band, plane - own] = piece[:, band * nx : (band + 1) * nx]
                split((level + 1) % 2, z * ny, planes * ny, new)
        for z, planes in blocks(own, own + thick):
            value, full = step(4, z, planes)
            new = (0.5 * half) * full + centre * value
            for plane in range(planes):
                piece = new[plane * ny : (plane + 1) * ny]
                for band in range(2):
                    image_ref[band, z + plane - own] = piece[:, band * nx : (band + 1) * nx]
        per = ny // 3
        for band in range(2):
            for z in range(thick):
                for f, at in enumerate((filt_ref.at[first + band, z], image_ref.at[band, z])):
                    for k in range(3):
                        line = ((z * per * bands + first + band) * 2 + f) * 3 + k
                        send_ref[pl.ds(line, per, stride=6 * bands), :] = at[pl.ds(k, per, stride=3), :]
        return carry

    lax.fori_loop(0, bands // 2, pair, 0)


def terms(value):
    lead = value.astype(jnp.bfloat16)
    return lead, (value - lead.astype(jnp.float32)).astype(jnp.bfloat16)


def gram_kernel(per_chunk, *refs):
    recv_refs, out_ref, held = refs[:-7], refs[-7], refs[-6:]
    size = held[0].shape[0]
    bands = per_chunk * len(recv_refs)
    groups = size // bands
    for f in range(2):
        for k in range(3):
            for band in range(bands):
                ref = recv_refs[band // per_chunk]
                first = ((band % per_chunk) * 2 + f) * 3 + k
                part = ref[pl.ds(first, groups, stride=6 * per_chunk), :]
                held[f * 3 + k][pl.ds(band, groups, stride=bands), :] = part
    filt, image = (
        terms(jnp.concatenate([ref[...] for ref in refs], axis=1)) for refs in (held[:3], held[3:])
    )
    right = jnp.concatenate([filt[0], filt[1], filt[0]], axis=1)
    for f, (lead, rest) in enumerate((filt, image)):
        block = lax.dot_general(
            jnp.concatenate([lead, lead, rest], axis=1),
            right,
            (((1,), (1,)), ((), ())),
            preferred_element_type=jnp.float32,
        )
        for c in range(2):
            out_ref[pl.ds(f * 2 + c, size, stride=4), :] = block[:, c * 128 : (c + 1) * 128]


def collect_kernel(recv_ref, out_ref):
    out_ref[...] = jnp.sum(recv_ref[...], axis=0)


def finish_kernel(volume, own_ref, near_ref, over_ref, far_ref, corr_ref, proj_ref):
    total = (own_ref[...] + over_ref[...]) + (near_ref[...] + far_ref[...])
    total = total * volume
    for band in range(corr_ref.shape[0]):
        for c in range(2):
            lanes = slice(c * 128, (c + 1) * 128)
            row = band * 4 + c
            corr_ref[band : band + 1, lanes] = total[row : row + 1]
            proj_ref[band : band + 1, lanes] = total[row + 2 : row + 3]


def shape(*dims):
    return jax.ShapeDtypeStruct(dims, jnp.float32)


def room(dims):
    kind = jnp.float32 if isinstance(dims[-1], int) else dims[-1]
    return pltpu.VMEM(tuple(d for d in dims if isinstance(d, int)), kind)


def call(kernel, outs, scratch=(), scalars=0):
    one = not isinstance(outs, tuple)

    def run(*args):
        return pl.pallas_call(
            kernel,
            out_shape=outs,
            in_specs=[pl.BlockSpec(memory_space=pltpu.SMEM)] * scalars + [VMEM] * (len(args) - scalars),
            out_specs=VMEM if one else (VMEM,) * len(outs),
            scratch_shapes=[room(dims) for dims in scratch],
            compiler_params=pltpu.CompilerParams(vmem_limit_bytes=16 * 2**20),
        )(*args)

    return run


def work(bands, potential):
    slabs = lax.axis_size("slab")
    groups = lax.axis_size("z") * lax.axis_size("y") * lax.axis_size("x")
    count, thick, ny, nx = bands.shape
    near = [(0, 1), (1, 0), (2, 3), (3, 2)]
    far = [(0, 3), (3, 0), (1, 2), (2, 1)]
    odd = jnp.reshape(lax.axis_index("slab") % 2, (1,)).astype(jnp.int32)
    rows = count * 2 * thick * ny

    pfar = lax.ppermute(potential, "slab", far)
    paired = bands.reshape(count, thick // 2, 2, ny, nx)
    outer = lax.ppermute(paired[:, :: thick // 2 - 1], "slab", far)
    inner = lax.ppermute(paired[:, 1:-1], "slab", far)
    beside = lax.ppermute(bands, "slab", near)
    pnear = lax.ppermute(potential, "slab", near)
    ends = lax.ppermute(outer, "slab", near)

    yz, x = (jnp.asarray(m, jnp.bfloat16) for m in stencil_matrices(ny, nx))
    deep = (3 * thick + 4) * ny + 64
    filtered, send = call(
        filter_kernel,
        (shape(count, thick, ny, nx), shape(rows, nx)),
        [
            (5, deep, 2 * nx),
            (2, 2, deep, 2 * nx, jnp.bfloat16),
            (2, thick, ny, nx),
            (deep, nx),
        ],
        scalars=1,
    )(odd, yz, x, beside, bands, outer, inner, ends, pnear, potential, pfar)
    swapped = lax.all_to_all(send.reshape(groups, -1, 2, nx), ("z", "y", "x"), 0, 0)
    received = swapped.reshape(rows, nx)

    size = groups * count
    parts = call(
        lambda *refs: gram_kernel(count, *refs), shape(size * 4, 128), [(size, nx)] * 6
    )(received)

    swapped = lax.all_to_all(parts.reshape(groups, count * 4, 128), ("z", "y", "x"), 0, 0)
    own = call(collect_kernel, shape(count * 4, 128))(swapped)
    over = [(i, (i + 2) % slabs) for i in range(slabs)]
    distant = lax.ppermute(own, "slab", far)
    opposite = lax.ppermute(own, "slab", over)
    sibling = lax.ppermute(own, "slab", near)
    volume = 1.0 / (slabs * thick * ny * nx)
    correlation, projected = call(
        lambda *refs: finish_kernel(volume, *refs), (shape(count, 2 * 128), shape(count, 2 * 128))
    )(own, sibling, opposite, distant)
    return filtered, correlation, projected


def solution(mesh):
    bands, slabs = mesh.devices.shape
    fine = Mesh(mesh.devices.reshape(bands // 8, 4, 2, slabs), ("z", "y", "x", "slab"))
    along = ("z", "y", "x")
    in_specs = (P(along, "slab", None, None), P("slab", None, None))
    out_specs = (P(along, "slab", None, None), P(along, None), P(along, None))
    return jax.shard_map(work, mesh=fine, in_specs=in_specs, out_specs=out_specs, check_vma=False)
```

```python
import jax
import jax.numpy as jnp
import numpy as np
from jax import lax
from jax.experimental import pallas as pl
from jax.experimental.pallas import tpu as pltpu
from jax.sharding import Mesh, PartitionSpec as P


centre = 4.5
half = 3.5
scale = 2.0 / half

VMEM = pl.BlockSpec(memory_space=pltpu.VMEM)


BLOCK = 6


def stencil_matrices(ny, nx):
    depth = -(-(BLOCK + 4) * ny // 128) * 128
    yz = np.zeros((BLOCK, ny, depth), np.float32)
    for plane in range(BLOCK):
        for y in range(ny):
            for step, weight in ((1, -16.0), (2, 1.0)):
                for sign in (-step, step):
                    yz[plane, y, (plane + 2 + sign) * ny + y] += weight
                    yz[plane, y, (plane + 2) * ny + (y + sign) % ny] += weight
    x = np.zeros((nx, nx), np.float32)
    for column in range(nx):
        for step, weight in ((1, -16.0), (2, 1.0)):
            for sign in (-step, step):
                x[(column + sign) % nx, column] += weight
    return yz.reshape(BLOCK * ny, depth), np.concatenate([x, x])


def blocks(low, high):
    return [(z, min(BLOCK, high - z)) for z in range(low, high, BLOCK)]


def filter_kernel(odd_ref, yz_ref, x_ref, near_ref, mid_ref, outer_ref, inner_ref, ends_ref, *rest):
    pnear_ref, pmid_ref, pfar_ref, *rest = rest
    thick = mid_ref.shape[1]

    def own(ref):
        return lambda band, z: ref[band, z]

    def far(band, z):
        if 2 <= z < thick - 2:
            return inner_ref[band, (z - 2) // 2, z % 2]
        return outer_ref[band, z // (thick - 2), z % 2]

    def ends(band, z):
        return ends_ref[band, z // 2, z % 2]

    odd = odd_ref[0]

    @pl.when(odd == 0)
    def _():
        fields, pots = (far, own(mid_ref), own(near_ref)), (pfar_ref, pmid_ref, pnear_ref)
        filter_bands(mid_ref.shape, yz_ref, x_ref, fields, ends, pots, *rest)

    @pl.when(odd == 1)
    def _():
        fields, pots = (own(near_ref), own(mid_ref), far), (pnear_ref, pmid_ref, pfar_ref)
        filter_bands(mid_ref.shape, yz_ref, x_ref, fields, ends, pots, *rest)


def filter_bands(
    dims, yz_ref, x_ref, fields, ends, pots,
    filt_ref, send_ref,
    field_ref, split_ref, image_ref, weight_ref,
):
    bands, thick, ny, nx = dims
    edge = 2
    total = 3 * thick + 2 * edge
    own = thick + edge
    depth = yz_ref.shape[1]
    pad = split_ref.shape[2] - total * ny

    for part, ref in enumerate(pots):
        for z in range(thick):
            top = (edge + part * thick + z) * ny
            weight_ref[top : top + ny, :] = (ref[z] + (3.75 - centre)) * scale

    def split(into, top, height, value):
        for term, part in enumerate(terms(value)):
            split_ref[into, term, top : top + height, :] = part

    blank = jnp.zeros((pad + 2 * ny, 2 * nx), jnp.bfloat16)
    for into in range(2):
        for term in range(2):
            split_ref[into, term, (total - 2) * ny :, :] = blank

    def dot(left, right):
        return jnp.dot(left, right, preferred_element_type=jnp.float32)

    def step(level, z, planes):
        source = level % 2
        window = slice((z - 2) * ny, (z - 2) * ny + depth)
        here = slice(z * ny, (z + planes) * ny)
        weights = yz_ref[: planes * ny, :]
        near = dot(weights, split_ref[source, 0, window, :])
        near = near + dot(weights, split_ref[source, 1, window, :])
        lead, rest = split_ref[source, 0, here, :], split_ref[source, 1, here, :]
        along = [
            dot(jnp.concatenate([lead[:, lanes], rest[:, lanes]], axis=1), x_ref[...])
            for lanes in (slice(0, nx), slice(nx, 2 * nx))
        ]
        near = near + jnp.concatenate(along, axis=1)
        value = field_ref[level, here, :]
        weight = weight_ref[here, :]
        weight = jnp.concatenate([weight, weight], axis=1)
        return value, weight * value + (scale / 24.0) * near

    def pair(index, carry):
        first = index * 2
        for z in range(0, total, 2):
            if z < edge:
                get, at = ends, z + edge
            elif z >= total - edge:
                get, at = ends, z - (total - edge)
            else:
                get, at = fields[(z - edge) // thick], (z - edge) % thick
            value = jnp.concatenate(
                [
                    jnp.concatenate([get(first + band, at), get(first + band, at + 1)], axis=0)
                    for band in range(2)
                ],
                axis=1,
            )
            field_ref[0, z * ny : (z + 2) * ny, :] = value
            split(0, z * ny, 2 * ny, value)
        for level in range(4):
            for z, planes in blocks(2 * level + 2, total - 2 * level - 2):
                here = slice(z * ny, (z + planes) * ny)
                full = step(level, z, planes)[1]
                new = 0.5 * full if level == 0 else full - field_ref[level - 1, here, :]
                if level < 3:
                    field_ref[level + 1, here, :] = new
                else:
                    field_ref[4, here, :] = new
                    for plane in range(max(z, own), min(z + planes, own + thick)):
                        piece = new[(plane - z) * ny : (plane - z + 1) * ny]
                        for band in range(2):
                            filt_ref[first + band, plane - own] = piece[:, band * nx : (band + 1) * nx]
                split((level + 1) % 2, z * ny, planes * ny, new)
        for z, planes in blocks(own, own + thick):
            value, full = step(4, z, planes)
            new = (0.5 * half) * full + centre * value
            for plane in range(planes):
                piece = new[plane * ny : (plane + 1) * ny]
                for band in range(2):
                    image_ref[band, z + plane - own] = piece[:, band * nx : (band + 1) * nx]
        per = ny // 3
        for band in range(2):
            for z in range(thick):
                for f, at in enumerate((filt_ref.at[first + band, z], image_ref.at[band, z])):
                    for k in range(3):
                        line = ((z * per * bands + first + band) * 2 + f) * 3 + k
                        send_ref[pl.ds(line, per, stride=6 * bands), :] = at[pl.ds(k, per, stride=3), :]
        return carry

    lax.fori_loop(0, bands // 2, pair, 0)


def terms(value):
    lead = value.astype(jnp.bfloat16)
    return lead, (value - lead.astype(jnp.float32)).astype(jnp.bfloat16)


def gram_kernel(bands, odd_ref, recv_ref, own_ref, other_ref, *held):
    size = held[0].shape[0]
    groups, part_size = size // bands, size // 2
    odd = odd_ref[0]
    for f in range(2):
        for k in range(3):
            for band in range(bands):
                part = recv_ref[pl.ds((band * 2 + f) * 3 + k, groups, stride=6 * bands), :]
                if f == 0:
                    held[k][pl.ds(band, groups, stride=bands), :] = part
                other = odd if band < 2 else 1 - odd
                rows = pl.ds(other * part_size + band % 2, groups, stride=2)
                held[3 + f * 3 + k][rows, :] = part
    right, filt, image = (
        terms(jnp.concatenate([ref[...] for ref in held[i : i + 3]], axis=1)) for i in (0, 3, 6)
    )
    right = jnp.concatenate([right[0], right[1], right[0]], axis=1)
    for f, (lead, rest) in enumerate((filt, image)):
        block = lax.dot_general(
            jnp.concatenate([lead, lead, rest], axis=1),
            right,
            (((1,), (1,)), ((), ())),
            preferred_element_type=jnp.float32,
        )
        for c in range(2):
            for i, ref in enumerate((own_ref, other_ref)):
                piece = block[i * part_size : (i + 1) * part_size, c * 128 : (c + 1) * 128]
                ref[pl.ds(f * 2 + c, part_size, stride=4), :] = piece


def collect_kernel(recv_ref, out_ref):
    out_ref[...] = jnp.sum(recv_ref[...], axis=0)


def finish_kernel(volume, odd_ref, own_ref, near_ref, over_ref, far_ref, corr_ref, proj_ref):
    odd = odd_ref[0]
    mine = (own_ref[...] + over_ref[...]) * volume
    theirs = (near_ref[...] + far_ref[...]) * volume
    for part in range(2):
        total = jnp.where(odd == part, mine, theirs)
        for line in range(2):
            for c in range(2):
                lanes = slice(c * 128, (c + 1) * 128)
                row, band = line * 4 + c, part * 2 + line
                corr_ref[band : band + 1, lanes] = total[row : row + 1]
                proj_ref[band : band + 1, lanes] = total[row + 2 : row + 3]


def shape(*dims):
    return jax.ShapeDtypeStruct(dims, jnp.float32)


def room(dims):
    kind = jnp.float32 if isinstance(dims[-1], int) else dims[-1]
    return pltpu.VMEM(tuple(d for d in dims if isinstance(d, int)), kind)


def call(kernel, outs, scratch=(), scalars=0):
    one = not isinstance(outs, tuple)

    def run(*args):
        return pl.pallas_call(
            kernel,
            out_shape=outs,
            in_specs=[pl.BlockSpec(memory_space=pltpu.SMEM)] * scalars + [VMEM] * (len(args) - scalars),
            out_specs=VMEM if one else (VMEM,) * len(outs),
            scratch_shapes=[room(dims) for dims in scratch],
            compiler_params=pltpu.CompilerParams(vmem_limit_bytes=16 * 2**20),
        )(*args)

    return run


def work(bands, potential):
    slabs = lax.axis_size("slab")
    groups = lax.axis_size("z") * lax.axis_size("y") * lax.axis_size("x")
    count, thick, ny, nx = bands.shape
    near = [(0, 1), (1, 0), (2, 3), (3, 2)]
    far = [(0, 3), (3, 0), (1, 2), (2, 1)]
    odd = jnp.reshape(lax.axis_index("slab") % 2, (1,)).astype(jnp.int32)
    rows = count * 2 * thick * ny

    pfar = lax.ppermute(potential, "slab", far)
    paired = bands.reshape(count, thick // 2, 2, ny, nx)
    outer = lax.ppermute(paired[:, :: thick // 2 - 1], "slab", far)
    inner = lax.ppermute(paired[:, 1:-1], "slab", far)
    beside = lax.ppermute(bands, "slab", near)
    pnear = lax.ppermute(potential, "slab", near)
    ends = lax.ppermute(outer, "slab", near)

    yz, x = (jnp.asarray(m, jnp.bfloat16) for m in stencil_matrices(ny, nx))
    deep = (3 * thick + 4) * ny + 64
    filtered, send = call(
        filter_kernel,
        (shape(count, thick, ny, nx), shape(rows, nx)),
        [
            (5, deep, 2 * nx),
            (2, 2, deep, 2 * nx, jnp.bfloat16),
            (2, thick, ny, nx),
            (deep, nx),
        ],
        scalars=1,
    )(odd, yz, x, beside, bands, outer, inner, ends, pnear, potential, pfar)
    swapped = lax.all_to_all(send.reshape(groups, -1, 2, nx), ("z", "y", "x"), 0, 0)
    received = swapped.reshape(rows, nx)

    size = groups * count
    halves = shape(size * 2, 128)
    mine, theirs = call(
        lambda *refs: gram_kernel(count, *refs), (halves, halves), [(size, nx)] * 9, scalars=1
    )(odd, received)
    parts = mine + lax.ppermute(theirs, "slab", near)

    swapped = lax.all_to_all(parts.reshape(groups, count * 2, 128), ("z", "y", "x"), 0, 0)
    own = call(collect_kernel, shape(count * 2, 128))(swapped)
    over = [(i, (i + 2) % slabs) for i in range(slabs)]
    distant = lax.ppermute(own, "slab", far)
    opposite = lax.ppermute(own, "slab", over)
    sibling = lax.ppermute(own, "slab", near)
    volume = 1.0 / (slabs * thick * ny * nx)
    correlation, projected = call(
        lambda *refs: finish_kernel(volume, *refs),
        (shape(count, 2 * 128), shape(count, 2 * 128)),
        scalars=1,
    )(odd, own, sibling, opposite, distant)
    return filtered, correlation, projected


def solution(mesh):
    bands, slabs = mesh.devices.shape
    fine = Mesh(mesh.devices.reshape(bands // 8, 4, 2, slabs), ("z", "y", "x", "slab"))
    along = ("z", "y", "x")
    in_specs = (P(along, "slab", None, None), P("slab", None, None))
    out_specs = (P(along, "slab", None, None), P(along, None), P(along, None))
    return jax.shard_map(work, mesh=fine, in_specs=in_specs, out_specs=out_specs, check_vma=False)
```

```python
import jax
import jax.numpy as jnp
import numpy as np
from jax import lax
from jax.experimental import pallas as pl
from jax.experimental.pallas import tpu as pltpu
from jax.sharding import Mesh, PartitionSpec as P


centre = 4.5
half = 3.5
scale = 2.0 / half

VMEM = pl.BlockSpec(memory_space=pltpu.VMEM)


BLOCK = 6


def stencil_matrices(ny, nx):
    depth = -(-(BLOCK + 4) * ny // 128) * 128
    yz = np.zeros((BLOCK, ny, depth), np.float32)
    for plane in range(BLOCK):
        for y in range(ny):
            for step, weight in ((1, -16.0), (2, 1.0)):
                for sign in (-step, step):
                    yz[plane, y, (plane + 2 + sign) * ny + y] += weight
                    yz[plane, y, (plane + 2) * ny + (y + sign) % ny] += weight
    x = np.zeros((nx, nx), np.float32)
    for column in range(nx):
        for step, weight in ((1, -16.0), (2, 1.0)):
            for sign in (-step, step):
                x[(column + sign) % nx, column] += weight
    return yz.reshape(BLOCK * ny, depth), np.concatenate([x, x])


def blocks(low, high):
    return [(z, min(BLOCK, high - z)) for z in range(low, high, BLOCK)]


def filter_kernel(odd_ref, yz_ref, x_ref, near_ref, mid_ref, outer_ref, inner_ref, ends_ref, *rest):
    pnear_ref, pmid_ref, pfar_ref, *rest = rest
    thick = mid_ref.shape[1]

    def own(ref):
        return lambda band, z: ref[band, z]

    def far(band, z):
        if 2 <= z < thick - 2:
            return inner_ref[band, (z - 2) // 2, z % 2]
        return outer_ref[band, z // (thick - 2), z % 2]

    def ends(band, z):
        return ends_ref[band, z // 2, z % 2]

    odd = odd_ref[0]

    @pl.when(odd == 0)
    def _():
        fields, pots = (far, own(mid_ref), own(near_ref)), (pfar_ref, pmid_ref, pnear_ref)
        filter_bands(mid_ref.shape, yz_ref, x_ref, fields, ends, pots, *rest)

    @pl.when(odd == 1)
    def _():
        fields, pots = (own(near_ref), own(mid_ref), far), (pnear_ref, pmid_ref, pfar_ref)
        filter_bands(mid_ref.shape, yz_ref, x_ref, fields, ends, pots, *rest)


def filter_bands(
    dims, yz_ref, x_ref, fields, ends, pots,
    filt_ref, send_ref,
    field_ref, split_ref, image_ref, weight_ref,
):
    bands, thick, ny, nx = dims
    edge = 2
    total = 3 * thick + 2 * edge
    own = thick + edge
    depth = yz_ref.shape[1]
    pad = split_ref.shape[2] - total * ny

    for part, ref in enumerate(pots):
        for z in range(thick):
            top = (edge + part * thick + z) * ny
            weight_ref[top : top + ny, :] = (ref[z] + (3.75 - centre)) * scale

    def split(into, top, height, value):
        for term, part in enumerate(terms(value)):
            split_ref[into, term, top : top + height, :] = part

    blank = jnp.zeros((pad + 2 * ny, 2 * nx), jnp.bfloat16)
    for into in range(2):
        for term in range(2):
            split_ref[into, term, (total - 2) * ny :, :] = blank

    def dot(left, right):
        return jnp.dot(left, right, preferred_element_type=jnp.float32)

    def step(level, z, planes):
        source = level % 2
        window = slice((z - 2) * ny, (z - 2) * ny + depth)
        here = slice(z * ny, (z + planes) * ny)
        weights = yz_ref[: planes * ny, :]
        near = dot(weights, split_ref[source, 0, window, :])
        near = near + dot(weights, split_ref[source, 1, window, :])
        lead, rest = split_ref[source, 0, here, :], split_ref[source, 1, here, :]
        halves = [
            jnp.concatenate([lead[:, lanes], rest[:, lanes]], axis=1)
            for lanes in (slice(0, nx), slice(nx, 2 * nx))
        ]
        along = dot(jnp.concatenate(halves, axis=0), x_ref[...])
        near = near + jnp.concatenate([along[: planes * ny], along[planes * ny :]], axis=1)
        value = field_ref[level, here, :]
        weight = weight_ref[here, :]
        weight = jnp.concatenate([weight, weight], axis=1)
        return value, weight * value + (scale / 24.0) * near

    def pair(index, carry):
        first = index * 2
        for z in range(0, total, 2):
            if z < edge:
                get, at = ends, z + edge
            elif z >= total - edge:
                get, at = ends, z - (total - edge)
            else:
                get, at = fields[(z - edge) // thick], (z - edge) % thick
            value = jnp.concatenate(
                [
                    jnp.concatenate([get(first + band, at), get(first + band, at + 1)], axis=0)
                    for band in range(2)
                ],
                axis=1,
            )
            field_ref[0, z * ny : (z + 2) * ny, :] = value
            split(0, z * ny, 2 * ny, value)
        for level in range(4):
            for z, planes in blocks(2 * level + 2, total - 2 * level - 2):
                here = slice(z * ny, (z + planes) * ny)
                full = step(level, z, planes)[1]
                new = 0.5 * full if level == 0 else full - field_ref[level - 1, here, :]
                if level < 3:
                    field_ref[level + 1, here, :] = new
                else:
                    field_ref[4, here, :] = new
                    for plane in range(max(z, own), min(z + planes, own + thick)):
                        piece = new[(plane - z) * ny : (plane - z + 1) * ny]
                        for band in range(2):
                            filt_ref[first + band, plane - own] = piece[:, band * nx : (band + 1) * nx]
                split((level + 1) % 2, z * ny, planes * ny, new)
        for z, planes in blocks(own, own + thick):
            value, full = step(4, z, planes)
            new = (0.5 * half) * full + centre * value
            for plane in range(planes):
                piece = new[plane * ny : (plane + 1) * ny]
                for band in range(2):
                    image_ref[band, z + plane - own] = piece[:, band * nx : (band + 1) * nx]
        per = ny // 3
        for band in range(2):
            for z in range(thick):
                for f, at in enumerate((filt_ref.at[first + band, z], image_ref.at[band, z])):
                    for k in range(3):
                        line = ((z * per * bands + first + band) * 2 + f) * 3 + k
                        send_ref[pl.ds(line, per, stride=6 * bands), :] = at[pl.ds(k, per, stride=3), :]
        return carry

    lax.fori_loop(0, bands // 2, pair, 0)


def terms(value):
    lead = value.astype(jnp.bfloat16)
    return lead, (value - lead.astype(jnp.float32)).astype(jnp.bfloat16)


def gram_kernel(bands, odd_ref, recv_ref, own_ref, other_ref, *held):
    size = held[0].shape[0]
    groups, part_size = size // bands, size // 2
    odd = odd_ref[0]
    for f in range(2):
        for k in range(3):
            for band in range(bands):
                part = recv_ref[pl.ds((band * 2 + f) * 3 + k, groups, stride=6 * bands), :]
                if f == 0:
                    held[k][pl.ds(band, groups, stride=bands), :] = part
                other = odd if band < 2 else 1 - odd
                rows = pl.ds(other * part_size + band % 2, groups, stride=2)
                held[3 + f * 3 + k][rows, :] = part
    right, filt, image = (
        terms(jnp.concatenate([ref[...] for ref in held[i : i + 3]], axis=1)) for i in (0, 3, 6)
    )
    right = jnp.concatenate([right[0], right[1], right[0]], axis=1)
    for f, (lead, rest) in enumerate((filt, image)):
        block = lax.dot_general(
            jnp.concatenate([lead, lead, rest], axis=1),
            right,
            (((1,), (1,)), ((), ())),
            preferred_element_type=jnp.float32,
        )
        for c in range(2):
            for i, ref in enumerate((own_ref, other_ref)):
                piece = block[i * part_size : (i + 1) * part_size, c * 128 : (c + 1) * 128]
                ref[pl.ds(f * 2 + c, part_size, stride=4), :] = piece


def collect_kernel(recv_ref, out_ref):
    out_ref[...] = jnp.sum(recv_ref[...], axis=0)


def finish_kernel(volume, odd_ref, own_ref, near_ref, over_ref, far_ref, corr_ref, proj_ref):
    odd = odd_ref[0]
    mine = (own_ref[...] + over_ref[...]) * volume
    theirs = (near_ref[...] + far_ref[...]) * volume
    for part in range(2):
        total = jnp.where(odd == part, mine, theirs)
        for line in range(2):
            for c in range(2):
                lanes = slice(c * 128, (c + 1) * 128)
                row, band = line * 4 + c, part * 2 + line
                corr_ref[band : band + 1, lanes] = total[row : row + 1]
                proj_ref[band : band + 1, lanes] = total[row + 2 : row + 3]


def shape(*dims):
    return jax.ShapeDtypeStruct(dims, jnp.float32)


def room(dims):
    kind = jnp.float32 if isinstance(dims[-1], int) else dims[-1]
    return pltpu.VMEM(tuple(d for d in dims if isinstance(d, int)), kind)


def call(kernel, outs, scratch=(), scalars=0):
    one = not isinstance(outs, tuple)

    def run(*args):
        return pl.pallas_call(
            kernel,
            out_shape=outs,
            in_specs=[pl.BlockSpec(memory_space=pltpu.SMEM)] * scalars + [VMEM] * (len(args) - scalars),
            out_specs=VMEM if one else (VMEM,) * len(outs),
            scratch_shapes=[room(dims) for dims in scratch],
            compiler_params=pltpu.CompilerParams(vmem_limit_bytes=16 * 2**20),
        )(*args)

    return run


def work(bands, potential):
    slabs = lax.axis_size("slab")
    groups = lax.axis_size("z") * lax.axis_size("y") * lax.axis_size("x")
    count, thick, ny, nx = bands.shape
    near = [(0, 1), (1, 0), (2, 3), (3, 2)]
    far = [(0, 3), (3, 0), (1, 2), (2, 1)]
    odd = jnp.reshape(lax.axis_index("slab") % 2, (1,)).astype(jnp.int32)
    rows = count * 2 * thick * ny

    pfar = lax.ppermute(potential, "slab", far)
    paired = bands.reshape(count, thick // 2, 2, ny, nx)
    outer = lax.ppermute(paired[:, :: thick // 2 - 1], "slab", far)
    middle = lax.optimization_barrier((paired, odd))[0][:, 1:-1]
    inner = lax.ppermute(middle, "slab", far)
    beside = lax.ppermute(bands, "slab", near)
    pnear = lax.ppermute(potential, "slab", near)
    ends = lax.ppermute(outer, "slab", near)

    yz, x = (jnp.asarray(m, jnp.bfloat16) for m in stencil_matrices(ny, nx))
    deep = (3 * thick + 4) * ny + 64
    filtered, send = call(
        filter_kernel,
        (shape(count, thick, ny, nx), shape(rows, nx)),
        [
            (5, deep, 2 * nx),
            (2, 2, deep, 2 * nx, jnp.bfloat16),
            (2, thick, ny, nx),
            (deep, nx),
        ],
        scalars=1,
    )(odd, yz, x, beside, bands, outer, inner, ends, pnear, potential, pfar)
    swapped = lax.all_to_all(send.reshape(groups, -1, 2, nx), ("z", "y", "x"), 0, 0)
    received = swapped.reshape(rows, nx)

    size = groups * count
    halves = shape(size * 2, 128)
    mine, theirs = call(
        lambda *refs: gram_kernel(count, *refs), (halves, halves), [(size, nx)] * 9, scalars=1
    )(odd, received)
    parts = mine + lax.ppermute(theirs, "slab", near)

    swapped = lax.all_to_all(parts.reshape(groups, count * 2, 128), ("z", "y", "x"), 0, 0)
    own = call(collect_kernel, shape(count * 2, 128))(swapped)
    over = [(i, (i + 2) % slabs) for i in range(slabs)]
    distant = lax.ppermute(own, "slab", far)
    opposite = lax.ppermute(own, "slab", over)
    sibling = lax.ppermute(own, "slab", near)
    volume = 1.0 / (slabs * thick * ny * nx)
    correlation, projected = call(
        lambda *refs: finish_kernel(volume, *refs),
        (shape(count, 2 * 128), shape(count, 2 * 128)),
        scalars=1,
    )(odd, own, sibling, opposite, distant)
    return filtered, correlation, projected


def solution(mesh):
    bands, slabs = mesh.devices.shape
    fine = Mesh(mesh.devices.reshape(bands // 8, 4, 2, slabs), ("z", "y", "x", "slab"))
    along = ("z", "y", "x")
    in_specs = (P(along, "slab", None, None), P("slab", None, None))
    out_specs = (P(along, "slab", None, None), P(along, None), P(along, None))
    return jax.shard_map(work, mesh=fine, in_specs=in_specs, out_specs=out_specs, check_vma=False)
```
